32 devices in a mesh: seq: 8 (over z, x), head: 4 (over y, core).
Axes of the slice: x: 2, y: 2, z: 4, core: 2. Of those that a mesh axis runs over, the one named last changes fastest.
Arguments:
- hidden: bfloat16 [8192, 8192], P('seq'), may hold values from -27 to 27, as said below
- key_value_weight: bfloat16 [8192, 2048], P('seq', 'head'), may hold values from -0.0625 to 0.0625
- down_projection: bfloat16 [2048, 512], P('head'), may hold values from -0.125 to 0.125
- up_projection: bfloat16 [512, 2048], P(None, 'head'), may hold values from -0.25 to 0.25
- positions: int32 [8192], P('seq'), may hold values from 0 to 131071
Outputs:
- grad_down: float32 [512, 2048], P('seq', 'head')
- grad_up: float32 [512, 2048], P('seq', 'head')
- rel_error: float32 [], replicated
The draws below stay inside these ranges and needn't reach their ends.
Inputs may be any that keep to these rules, and one draw needn't show every extreme that they name: `hidden`: real-valued inputs, rows of differing scale.
All inputs are finite; a program needn't handle non-finite values.
Results may differ from the reference program's by a relative error of at most 0.0045.
Values may be sent and summed in bfloat16 or wider, within the bound.
A program may use at most 64 MiB of HBM per device.

```python
import math
import jax
import jax.numpy as jnp
from jax import lax

MODEL_WIDTH = 8192
KEY_VALUE_HEADS = 8
HEAD_SIZE = 128
LATENT_RANK = 512
WINDOW_TOKENS = 8192


def draw_hidden(key, part):
    first_key, second_key = jax.random.split(key, 2)
    row_index = jnp.arange(WINDOW_TOKENS, dtype=jnp.float32)
    row_scale = jnp.exp(jax.random.uniform(second_key, (WINDOW_TOKENS, 1), jnp.float32, jnp.log(0.3), jnp.log(3.0)))
    base = jnp.clip(jax.random.normal(first_key, (WINDOW_TOKENS, MODEL_WIDTH), jnp.float32), -6.0, 6.0)
    ramp = 1.0 + 0.75 * row_index / WINDOW_TOKENS
    return (base * row_scale * ramp[:, None]).astype(jnp.bfloat16)


def plant(array, stream_key, smallest, top_value):
    spot = [jax.random.randint(jax.random.fold_in(stream_key, axis), (), 0, length) for axis, length in enumerate(array.shape)]
    widest = array.shape.index(max(array.shape))
    neighbour = spot[:widest] + [(spot[widest] + 1) % array.shape[widest]] + spot[widest + 1:]
    return array.at[tuple(spot)].set(smallest).at[tuple(neighbour)].set(top_value)


def block_scale(key, extent, cuts, low, largest):
    def one(dim, blocks):
        steps = jax.random.uniform(jax.random.fold_in(jax.random.fold_in(key, 6), dim), (blocks,), jnp.float32, low / len(cuts), largest / len(cuts))
        return jnp.repeat(jnp.exp(steps), extent[dim] // blocks).reshape((-1,) + (1,) * (len(extent) - dim - 1))

    factor_of = one(*cuts[0])
    for cut in cuts[1:]:
        factor_of = factor_of * one(*cut)
    return factor_of


def gaussian(own_key, dims, deviation, limit, cuts=(), kind=jnp.bfloat16):
    array = jax.random.normal(own_key, dims, jnp.float32) * deviation
    if len(cuts) > 0:
        array = block_scale(own_key, dims, cuts, -0.22, 0.18) * array
    return jnp.clip(array, min=-limit, max=limit).astype(kind)


def setup_inputs(seed: int = 0) -> dict:
    arg_keys = jax.random.split(jax.random.key(seed), 6)
    hidden = draw_hidden(jax.random.fold_in(arg_keys[5], 71), 0)
    key_value_weight = gaussian(arg_keys[1], (MODEL_WIDTH, 2 * KEY_VALUE_HEADS * HEAD_SIZE), MODEL_WIDTH ** -0.5, 0.0625, ((0, 8), (1, 4)))
    down_projection = gaussian(arg_keys[2], (2 * KEY_VALUE_HEADS * HEAD_SIZE, LATENT_RANK), (2 * KEY_VALUE_HEADS * HEAD_SIZE) ** -0.5, 0.125, ((0, 4),))
    up_projection = gaussian(arg_keys[3], (LATENT_RANK, 2 * KEY_VALUE_HEADS * HEAD_SIZE), LATENT_RANK ** -0.5, 0.25, ((1, 4),))
    positions = plant(jax.random.randint(arg_keys[4], (WINDOW_TOKENS,), 0, 131072), jax.random.fold_in(arg_keys[4], 1), 0, 131071).astype(jnp.int32)
    return {"hidden": hidden, "key_value_weight": key_value_weight, "down_projection": down_projection, "up_projection": up_projection, "positions": positions}


THETA = 500000.0

def rotate_targets(dense, positions):
    half_dim = HEAD_SIZE // 2
    freqs = jnp.power(jnp.float32(THETA), -(jnp.arange(half_dim, dtype=jnp.float32) * 2.0 / HEAD_SIZE))
    angle = positions.astype(jnp.float32)[:, None] * freqs[None, :]
    cosine = jnp.cos(angle)[:, None, :]
    sine = jnp.sin(angle)[:, None, :]
    shaped = dense.reshape(dense.shape[0], -1, 2, HEAD_SIZE)
    key_part = shaped[:, :, 0, :]
    first = key_part[..., :half_dim]
    second = key_part[..., half_dim:]
    turned = jnp.concatenate([first * cosine - second * sine, second * cosine + first * sine], axis=-1)
    joined = jnp.stack([turned, shaped[:, :, 1, :]], axis=2)
    return joined.reshape(dense.shape[0], -1).astype(jnp.bfloat16)

def reference(hidden, key_value_weight, down_projection, up_projection, positions):
    dense = jnp.dot(hidden, key_value_weight, preferred_element_type=jnp.float32)
    targets = rotate_targets(dense, positions)
    target_wide = targets.astype(jnp.float32)
    energy = jnp.sum(target_wide * target_wide)
    latent = jnp.dot(targets, down_projection, preferred_element_type=jnp.float32).astype(jnp.bfloat16)
    rebuilt = jnp.dot(latent, up_projection, preferred_element_type=jnp.float32)
    residual = target_wide - rebuilt
    rel_error = jnp.sum(residual * residual) / energy
    entry_items = WINDOW_TOKENS * 2 * KEY_VALUE_HEADS * HEAD_SIZE
    factor = -(entry_items / energy) / math.sqrt(WINDOW_TOKENS)
    latent_wide = latent.astype(jnp.float32)
    up_wide = up_projection.astype(jnp.float32)
    grad_up = factor * jnp.dot(latent_wide.T, residual, precision=lax.Precision.HIGHEST, preferred_element_type=jnp.float32)
    d_latent = jnp.dot(residual, up_wide.T, precision=lax.Precision.HIGHEST, preferred_element_type=jnp.float32).astype(jnp.bfloat16)
    grad_down = factor * jnp.dot(d_latent.T, targets, preferred_element_type=jnp.float32)
    return (grad_down, grad_up, rel_error)
```

```python
import functools
import math

import jax
import jax.numpy as jnp
from jax import lax
from jax.experimental import pallas as pl
from jax.experimental.pallas import tpu as pltpu
from jax.sharding import PartitionSpec as P

KEY_VALUE_HEADS = 8
HEAD_SIZE = 128
THETA = 500000.0
MESH = pl.DeviceIdType.MESH
BF16 = jnp.bfloat16
F32 = jnp.float32


def rotation(positions):
    half_dim = HEAD_SIZE // 2
    freqs = jnp.power(
        jnp.float32(THETA), -(jnp.arange(half_dim, dtype=jnp.float32) * 2.0 / HEAD_SIZE)
    )
    angle = positions.astype(jnp.float32)[:, None] * freqs[None, :]
    cosine = jnp.cos(angle)
    sine = jnp.sin(angle)
    return (
        jnp.concatenate([cosine, cosine], axis=-1),
        jnp.concatenate([-sine, sine], axis=-1),
    )


def gather_kernel(
    A, B, chunks, minor_first,
    hidden_ref, weight_ref, cos_ref, sin_ref, out_ref,
    hid, wbuf, acc, hid_sem, own_sem, send_sem, recv_sem,
):
    s, h = lax.axis_index("seq"), lax.axis_index("head")
    a, b = s // B, s % B
    depth = hid.shape[1] // (A * B)
    cols = weight_ref.shape[-1]
    load = pltpu.make_async_copy(hidden_ref, hid, hid_sem)
    load.start()
    own = pltpu.make_async_copy(weight_ref, wbuf.at[s], own_sem)
    own.start()

    barrier = pltpu.get_barrier_semaphore()
    ways = (
        (a + 1 < A, s + B),
        (a > 0, s - B),
        (b + 1 < B, s + 1),
        (b > 0, s - 1),
    )
    for there, peer in ways:
        @pl.when(there)
        def _():
            pl.semaphore_signal(barrier, inc=1, device_id=(peer, h), device_id_type=MESH)
    met = sum(there.astype(jnp.int32) for there, _ in ways)
    pl.semaphore_wait(barrier, met)

    def copy(way, peer, o, i):
        return pltpu.make_async_remote_copy(
            src_ref=wbuf.at[o, i],
            dst_ref=wbuf.at[o, i],
            send_sem=send_sem.at[way, o, i],
            recv_sem=recv_sem.at[o, i],
            device_id=(peer, h),
            device_id_type=MESH,
        )

    def forwards(da, db, o, i, act):
        first = i < minor_first
        conds = (
            (da >= 0) & (first | (db == 0)),
            (da <= 0) & (first | (db == 0)),
            (db >= 0) & (jnp.logical_not(first) | (da == 0)),
            (db <= 0) & (jnp.logical_not(first) | (da == 0)),
        )
        for way in range(4):
            @pl.when(ways[way][0] & conds[way])
            def _():
                act(copy(way, ways[way][1], o, i))

    def product(o):
        start = pl.multiple_of(o * depth, depth)
        w = wbuf[o].reshape(depth, cols)
        rows = 256
        def tile(m, c):
            r = pl.ds(pl.multiple_of(m * rows, rows), rows)
            acc[r, :] += jnp.dot(hid[r, pl.ds(start, depth)], w, preferred_element_type=F32)
            return c
        lax.fori_loop(0, hid.shape[0] // rows, tile, 0)

    own.wait()

    def issue(i, c):
        forwards(0, 0, s, i, lambda d: d.start())
        return c
    lax.fori_loop(0, chunks, issue, 0)
    acc[...] = jnp.zeros_like(acc)
    load.wait()
    product(s)

    def combos(u):
        for e in range(B):
            for eb in ((1, -1) if e else (1,)):
                for sa in (1, -1):
                    yield e * eb, u + 1 - e, sa

    def each(u, act):
        for off_b, d, sa in combos(u):
            a0, b0 = a + sa * d, b + off_b
            ok = (d >= 0) & (a0 >= 0) & (a0 < A) & (b0 >= 0) & (b0 < B)
            if sa < 0:
                ok = ok & (d > 0)

            @pl.when(ok)
            def _():
                act(a - a0, b - b0, a0 * B + b0)

    def stage(u, c):
        def chunk(i, c):
            def arrive(da, db, o):
                copy(0, s, o, i).wait_recv()
                forwards(da, db, o, i, lambda d: d.start())
            each(u, arrive)
            return c
        lax.fori_loop(0, chunks, chunk, 0)
        each(u, lambda da, db, o: product(o))
        return c
    lax.fori_loop(0, A + B - 2, stage, 0)

    def finish(o, c):
        def chunk(i, c):
            forwards(a - o // B, b - o % B, o, i, lambda d: d.wait_send())
            return c
        return lax.fori_loop(0, chunks, chunk, c)
    lax.fori_loop(0, A * B, finish, 0)

    for head in range(cols // (2 * HEAD_SIZE)):
        k0 = head * 2 * HEAD_SIZE
        key = acc[:, k0 : k0 + HEAD_SIZE]
        turned = key * cos_ref[...] + pltpu.roll(key, HEAD_SIZE // 2, 1) * sin_ref[...]
        out_ref[:, k0 : k0 + HEAD_SIZE] = turned.astype(BF16)
        out_ref[:, k0 + HEAD_SIZE : k0 + 2 * HEAD_SIZE] = acc[
            :, k0 + HEAD_SIZE : k0 + 2 * HEAD_SIZE
        ].astype(BF16)


def gather_targets(N, hidden, weight, cosine, sine):
    B = 2 if N <= 8 else 8
    A = N // B
    rows, width = hidden.shape
    depth, cols = weight.shape
    chunks = 8 if N <= 8 else 2
    minor_first = 1 if N <= 8 else 0
    shard = (chunks, depth // chunks, cols)
    return pl.pallas_call(
        functools.partial(gather_kernel, A, B, chunks, minor_first),
        out_shape=jax.ShapeDtypeStruct((rows, cols), BF16),
        in_specs=[pl.BlockSpec(memory_space=pl.ANY)] * 2
        + [pl.BlockSpec(memory_space=pltpu.VMEM)] * 2,
        out_specs=pl.BlockSpec(memory_space=pltpu.VMEM),
        scratch_shapes=[
            pltpu.VMEM((rows, width), BF16),
            pltpu.VMEM((N,) + shard, BF16),
            pltpu.VMEM((rows, cols), F32),
            pltpu.SemaphoreType.DMA,
            pltpu.SemaphoreType.DMA,
            pltpu.SemaphoreType.DMA((4, N, chunks)),
            pltpu.SemaphoreType.DMA((N, chunks)),
        ],
        compiler_params=pltpu.CompilerParams(
            collective_id=0, has_side_effects=True, vmem_limit_bytes=50 * 2**20
        ),
    )(hidden, weight.reshape(shard), cosine, sine)


def tail_kernel(
    N, H, entry_items, token_count,
    t_ref, d_ref, u_ref, gd_ref, gu_ref, rel_ref,
    snd, rcv, own, ybuf, lat, dlat, res, gsend, grecv, eh, es,
    c_send, c_recv, y_send, y_recv, g_send, g_recv, eh_send, eh_recv, es_send, es_recv,
):
    s, h = lax.axis_index("seq"), lax.axis_index("head")
    Y = H // 2
    y, core = h // 2, h % 2
    other = 1 - core
    sib = y * 2 + other
    chunks, _, half, cols = t_ref.shape
    rank = d_ref.shape[1]

    barrier = pltpu.get_barrier_semaphore()
    for j in range(1, H):
        pl.semaphore_signal(barrier, inc=1, device_id=(s, (h + j) % H), device_id_type=MESH)
    for j in range(1, N):
        pl.semaphore_signal(barrier, inc=1, device_id=((s + j) % N, h), device_id_type=MESH)

    def remote(src, dst, ssem, rsem, peer):
        return pltpu.make_async_remote_copy(
            src_ref=src, dst_ref=dst, send_sem=ssem, recv_sem=rsem,
            device_id=peer, device_id_type=MESH,
        )

    def to_sib(g, k):
        return remote(snd.at[g, k], rcv.at[g, k], c_send.at[g, 0, k], c_recv.at[g, 0, k], (s, sib))

    def back(g, k, slot):
        buf = lat if g == 0 else dlat
        return remote(buf.at[k, slot], buf.at[k, slot], c_send.at[g, 1, k], c_recv.at[g, 1, k], (s, sib))

    def to_y(g, k, slot, yy):
        return remote(
            ybuf.at[g, k, slot], ybuf.at[g, k, slot], y_send.at[g, k, yy], y_recv.at[g, k, slot],
            (s, yy * 2 + core),
        )

    def to_seq(g, slot, ss):
        return remote(gsend.at[g, ss], grecv.at[g, slot], g_send.at[g, ss], g_recv.at[g, slot], (ss, h))

    def nt(x, w):
        return lax.dot_general(x, w, (((1,), (1,)), ((), ())), preferred_element_type=F32)

    def tn(x, w):
        return lax.dot_general(x, w, (((0,), (0,)), ((), ())), preferred_element_type=F32)

    energy = jnp.zeros((), F32)
    for k in range(chunks):
        snd[0, k] = jnp.dot(t_ref[k, other], d_ref[...], preferred_element_type=F32).astype(BF16)
        if k == 0:
            pl.semaphore_wait(barrier, H - 1 + N - 1)
        to_sib(0, k).start()

    def meet(g, k):
        to_sib(g, k).wait_recv()
        ybuf[g, k, y] = (own[k] + rcv[g, k].astype(F32)).astype(BF16)
        for j in range(1, Y):
            to_y(g, k, y, (y + j) % Y).start()

    for k in range(chunks):
        own[k] = jnp.dot(t_ref[k, core], d_ref[...], preferred_element_type=F32)
        meet(0, k)
    for k in range(chunks):
        for c in range(2):
            wide = t_ref[k, c].astype(F32)
            energy += jnp.sum(wide * wide)

    def joined(g, k):
        for j in range(1, Y):
            to_y(g, k, (y + j) % Y, (y + j) % Y).wait_recv()
        total = ybuf[g, k, 0].astype(F32)
        for yy in range(1, Y):
            total += ybuf[g, k, yy].astype(F32)
        buf = lat if g == 0 else dlat
        buf[k, core] = total.astype(BF16)
        back(g, k, core).start()

    def residual(k, c):
        r = t_ref[k, c].astype(F32) - jnp.dot(lat[k, c], u_ref[...], preferred_element_type=F32)
        res[k, c] = r.astype(BF16)
        return jnp.sum(r * r)

    misfit = jnp.zeros((), F32)
    for k in range(chunks):
        joined(0, k)
    for k in range(chunks):
        back(0, k, other).wait_recv()
        misfit += residual(k, other)
        snd[1, k] = nt(res[k, other], u_ref[...]).astype(BF16)
        to_sib(1, k).start()
    for k in range(chunks):
        misfit += residual(k, core)
        own[k] = nt(res[k, core], u_ref[...])
        meet(1, k)

    tile = eh.shape[-2:]
    eh[h, 0] = jnp.full(tile, energy, F32)
    eh[h, 1] = jnp.full(tile, misfit, F32)

    def to_head(slot, hh):
        return remote(eh.at[slot], eh.at[slot], eh_send.at[hh], eh_recv.at[slot], (s, hh))

    def to_all(slot, ss):
        return remote(es.at[slot], es.at[slot], es_send.at[ss], es_recv.at[slot], (ss, h))

    for j in range(1, H):
        to_head(h, (h + j) % H).start()

    def scatter(g, left, right):
        grad = tn(left[...].reshape(-1, rank), right[...].reshape(-1, cols))
        gsend[g] = grad.reshape(gsend.shape[1:]).astype(BF16)
        for j in range(1, N):
            ss = (s + j) % N
            to_seq(g, s, ss).start()

    scatter(0, lat, res)
    for j in range(1, H):
        hh = (h + j) % H
        to_head(hh, hh).wait_recv()
    total = eh[0]
    for hh in range(1, H):
        total += eh[hh]
    es[s] = total
    for j in range(1, N):
        to_all(s, (s + j) % N).start()

    for k in range(chunks):
        joined(1, k)
    for k in range(chunks):
        back(1, k, other).wait_recv()
    scatter(1, dlat, t_ref)

    for j in range(1, N):
        ss = (s + j) % N
        to_all(ss, ss).wait_recv()
    total = es[0]
    for ss in range(1, N):
        total += es[ss]
    whole_energy, whole_misfit = total[0], total[1]
    rel_ref[...] = whole_misfit / whole_energy
    factor = (-(entry_items / whole_energy) / math.sqrt(token_count))[0:1, 0:1]

    for g, out in ((0, gu_ref), (1, gd_ref)):
        total = gsend[g, s].astype(F32)
        for j in range(1, N):
            ss = (s + j) % N
            to_seq(g, ss, ss).wait_recv()
            total += grecv[g, ss].astype(F32)
        out[...] = factor * total

    for g in range(2):
        for k in range(chunks):
            to_sib(g, k).wait_send()
            back(g, k, core).wait_send()
            for j in range(1, Y):
                to_y(g, k, y, (y + j) % Y).wait_send()
        for j in range(1, N):
            to_seq(g, s, (s + j) % N).wait_send()
    for j in range(1, H):
        to_head(h, (h + j) % H).wait_send()
    for j in range(1, N):
        to_all(s, (s + j) % N).wait_send()


def tail(N, H, targets, down, up):
    rows, cols = targets.shape
    rank = down.shape[1]
    chunks = 4
    half = rows // chunks // 2
    block = rank // N
    Y = H // 2
    dma = pltpu.SemaphoreType.DMA
    vmem = pl.BlockSpec(memory_space=pltpu.VMEM)
    token_count = N * rows
    return pl.pallas_call(
        functools.partial(
            tail_kernel, N, H, token_count * 2 * KEY_VALUE_HEADS * HEAD_SIZE, token_count
        ),
        out_shape=(
            jax.ShapeDtypeStruct((block, cols), F32),
            jax.ShapeDtypeStruct((block, cols), F32),
            jax.ShapeDtypeStruct((8, 128), F32),
        ),
        in_specs=[vmem] * 3,
        out_specs=(vmem,) * 3,
        scratch_shapes=[
            pltpu.VMEM((2, chunks, half, rank), BF16),
            pltpu.VMEM((2, chunks, half, rank), BF16),
            pltpu.VMEM((chunks, half, rank), F32),
            pltpu.VMEM((2, chunks, Y, half, rank), BF16),
            pltpu.VMEM((chunks, 2, half, rank), BF16),
            pltpu.VMEM((chunks, 2, half, rank), BF16),
            pltpu.VMEM((chunks, 2, half, cols), BF16),
            pltpu.VMEM((2, N, block, cols), BF16),
            pltpu.VMEM((2, N, block, cols), BF16),
            pltpu.VMEM((H, 2, 8, 128), F32),
            pltpu.VMEM((N, 2, 8, 128), F32),
            dma((2, 2, chunks)),
            dma((2, 2, chunks)),
            dma((2, chunks, Y)),
            dma((2, chunks, Y)),
            dma((2, N)),
            dma((2, N)),
            dma((H,)),
            dma((H,)),
            dma((N,)),
            dma((N,)),
        ],
        compiler_params=pltpu.CompilerParams(
            collective_id=1, has_side_effects=True, vmem_limit_bytes=48 * 2**20
        ),
    )(targets.reshape(chunks, 2, half, cols), down, up)


def solution(mesh):
    N, H = mesh.shape["seq"], mesh.shape["head"]

    def per_device(hidden, key_value_weight, down_projection, up_projection, positions):
        cosine, sine = rotation(positions)
        targets = gather_targets(N, hidden, key_value_weight, cosine, sine)
        grad_down, grad_up, rel = tail(N, H, targets, down_projection, up_projection)
        return grad_down, grad_up, rel[0, 0]

    return jax.shard_map(
        per_device,
        mesh=mesh,
        in_specs=(P("seq", None), P("seq", "head"), P("head", None), P(None, "head"), P("seq")),
        out_specs=(P("seq", "head"), P("seq", "head"), P()),
        check_vma=False,
    )
```

```python
import functools
import math

import jax
import jax.numpy as jnp
from jax import lax
from jax.experimental import pallas as pl
from jax.experimental.pallas import tpu as pltpu
from jax.sharding import PartitionSpec as P

KEY_VALUE_HEADS = 8
HEAD_SIZE = 128
THETA = 500000.0
MESH = pl.DeviceIdType.MESH
BF16 = jnp.bfloat16
F32 = jnp.float32


def rotation(positions):
    half_dim = HEAD_SIZE // 2
    freqs = jnp.power(
        jnp.float32(THETA), -(jnp.arange(half_dim, dtype=jnp.float32) * 2.0 / HEAD_SIZE)
    )
    angle = positions.astype(jnp.float32)[:, None] * freqs[None, :]
    cosine = jnp.cos(angle)
    sine = jnp.sin(angle)
    return (
        jnp.concatenate([cosine, cosine], axis=-1),
        jnp.concatenate([-sine, sine], axis=-1),
    )


def gather_kernel(
    A, B, chunks, groups, minor_first,
    hidden_ref, weight_ref, cos_ref, sin_ref, out_ref,
    hid, wbuf, acc, hid_sem, own_sem, send_sem, recv_sem,
):
    s, h = lax.axis_index("seq"), lax.axis_index("head")
    a, b = s // B, s % B
    depth = hid.shape[1] // (A * B)
    cols = weight_ref.shape[-1]
    load = pltpu.make_async_copy(hidden_ref, hid, hid_sem)
    load.start()
    own = pltpu.make_async_copy(weight_ref, wbuf.at[s], own_sem)
    own.start()

    barrier = pltpu.get_barrier_semaphore()
    ways = (
        (a + 1 < A, s + B),
        (a > 0, s - B),
        (b + 1 < B, s + 1),
        (b > 0, s - 1),
    )
    for there, peer in ways:
        @pl.when(there)
        def _():
            pl.semaphore_signal(barrier, inc=1, device_id=(peer, h), device_id_type=MESH)
    met = sum(there.astype(jnp.int32) for there, _ in ways)
    pl.semaphore_wait(barrier, met)

    def copy(way, peer, o, i):
        return pltpu.make_async_remote_copy(
            src_ref=wbuf.at[o, i],
            dst_ref=wbuf.at[o, i],
            send_sem=send_sem.at[way, o, i],
            recv_sem=recv_sem.at[o, i],
            device_id=(peer, h),
            device_id_type=MESH,
        )

    def forwards(da, db, o, i, act):
        first = i < minor_first
        conds = (
            (da >= 0) & (first | (db == 0)),
            (da <= 0) & (first | (db == 0)),
            (db >= 0) & (jnp.logical_not(first) | (da == 0)),
            (db <= 0) & (jnp.logical_not(first) | (da == 0)),
        )
        for way in range(4):
            @pl.when(ways[way][0] & conds[way])
            def _():
                act(copy(way, ways[way][1], o, i))

    piece = depth // groups
    span = chunks // groups

    def product(o, q):
        start = pl.multiple_of(o * depth + q * piece, piece)
        w = wbuf[o, pl.ds(q * span, span)].reshape(piece, cols)
        rows = 256
        def tile(m, c):
            r = pl.ds(pl.multiple_of(m * rows, rows), rows)
            acc[r, :] += jnp.dot(hid[r, pl.ds(start, piece)], w, preferred_element_type=F32)
            return c
        lax.fori_loop(0, hid.shape[0] // rows, tile, 0)

    own.wait()

    def issue(i, c):
        forwards(0, 0, s, i, lambda d: d.start())
        return c
    lax.fori_loop(0, chunks, issue, 0)
    acc[...] = jnp.zeros_like(acc)
    load.wait()

    def own_product(q, c):
        product(s, q)
        return c
    lax.fori_loop(0, groups, own_product, 0)

    def combos(u):
        for e in range(B):
            for eb in ((1, -1) if e else (1,)):
                for sa in (1, -1):
                    yield e * eb, u + 1 - e, sa

    def each(u, act):
        for off_b, d, sa in combos(u):
            a0, b0 = a + sa * d, b + off_b
            ok = (d >= 0) & (a0 >= 0) & (a0 < A) & (b0 >= 0) & (b0 < B)
            if sa < 0:
                ok = ok & (d > 0)

            @pl.when(ok)
            def _():
                act(a - a0, b - b0, a0 * B + b0)

    def stage(u, c):
        def group(q, c):
            def chunk(j, c):
                i = q * span + j

                def arrive(da, db, o):
                    copy(0, s, o, i).wait_recv()
                    forwards(da, db, o, i, lambda d: d.start())
                each(u, arrive)
                return c
            lax.fori_loop(0, span, chunk, 0)
            each(u, lambda da, db, o: product(o, q))
            return c
        return lax.fori_loop(0, groups, group, c)
    lax.fori_loop(0, A + B - 2, stage, 0)

    def finish(o, c):
        def chunk(i, c):
            forwards(a - o // B, b - o % B, o, i, lambda d: d.wait_send())
            return c
        return lax.fori_loop(0, chunks, chunk, c)
    lax.fori_loop(0, A * B, finish, 0)

    for head in range(cols // (2 * HEAD_SIZE)):
        k0 = head * 2 * HEAD_SIZE
        key = acc[:, k0 : k0 + HEAD_SIZE]
        turned = key * cos_ref[...] + pltpu.roll(key, HEAD_SIZE // 2, 1) * sin_ref[...]
        out_ref[:, k0 : k0 + HEAD_SIZE] = turned.astype(BF16)
        out_ref[:, k0 + HEAD_SIZE : k0 + 2 * HEAD_SIZE] = acc[
            :, k0 + HEAD_SIZE : k0 + 2 * HEAD_SIZE
        ].astype(BF16)


def gather_targets(N, hidden, weight, cosine, sine):
    B = 2 if N <= 8 else 8
    A = N // B
    rows, width = hidden.shape
    depth, cols = weight.shape
    chunks = 16 if N <= 8 else 2
    groups = max(1, depth // 256)
    minor_first = 3 if N <= 8 else 0
    shard = (chunks, depth // chunks, cols)
    return pl.pallas_call(
        functools.partial(gather_kernel, A, B, chunks, groups, minor_first),
        out_shape=jax.ShapeDtypeStruct((rows, cols), BF16),
        in_specs=[pl.BlockSpec(memory_space=pl.ANY)] * 2
        + [pl.BlockSpec(memory_space=pltpu.VMEM)] * 2,
        out_specs=pl.BlockSpec(memory_space=pltpu.VMEM),
        scratch_shapes=[
            pltpu.VMEM((rows, width), BF16),
            pltpu.VMEM((N,) + shard, BF16),
            pltpu.VMEM((rows, cols), F32),
            pltpu.SemaphoreType.DMA,
            pltpu.SemaphoreType.DMA,
            pltpu.SemaphoreType.DMA((4, N, chunks)),
            pltpu.SemaphoreType.DMA((N, chunks)),
        ],
        compiler_params=pltpu.CompilerParams(
            collective_id=0, has_side_effects=True, vmem_limit_bytes=50 * 2**20
        ),
    )(hidden, weight.reshape(shard), cosine, sine)


def tail_kernel(
    N, H, entry_items, token_count,
    t_ref, d_ref, u_ref, gd_ref, gu_ref, rel_ref,
    snd, rcv, own, gacc, ybuf, lat, dlat, res, gsend, grecv, eh, es,
    c_send, c_recv, y_send, y_recv, g_send, g_recv, eh_send, eh_recv, es_send, es_recv,
):
    s, h = lax.axis_index("seq"), lax.axis_index("head")
    Y = H // 2
    y, core = h // 2, h % 2
    other = 1 - core
    sib = y * 2 + other
    chunks, _, half, cols = t_ref.shape
    rank = d_ref.shape[1]

    barrier = pltpu.get_barrier_semaphore()
    for j in range(1, H):
        pl.semaphore_signal(barrier, inc=1, device_id=(s, (h + j) % H), device_id_type=MESH)
    for j in range(1, N):
        pl.semaphore_signal(barrier, inc=1, device_id=((s + j) % N, h), device_id_type=MESH)

    def remote(src, dst, ssem, rsem, peer):
        return pltpu.make_async_remote_copy(
            src_ref=src, dst_ref=dst, send_sem=ssem, recv_sem=rsem,
            device_id=peer, device_id_type=MESH,
        )

    def to_sib(g, k):
        return remote(snd.at[g, k], rcv.at[g, k], c_send.at[g, 0, k], c_recv.at[g, 0, k], (s, sib))

    def back(g, k, slot):
        buf = lat if g == 0 else dlat
        return remote(buf.at[k, slot], buf.at[k, slot], c_send.at[g, 1, k], c_recv.at[g, 1, k], (s, sib))

    def to_y(g, k, slot, yy):
        return remote(
            ybuf.at[g, k, slot], ybuf.at[g, k, slot], y_send.at[g, k, yy], y_recv.at[g, k, slot],
            (s, yy * 2 + core),
        )

    def to_seq(g, slot, ss):
        return remote(gsend.at[g, ss], grecv.at[g, slot], g_send.at[g, ss], g_recv.at[g, slot], (ss, h))

    def nt(x, w):
        return lax.dot_general(x, w, (((1,), (1,)), ((), ())), preferred_element_type=F32)

    def tn(x, w):
        return lax.dot_general(x, w, (((0,), (0,)), ((), ())), preferred_element_type=F32)

    energy = jnp.zeros((), F32)
    for k in range(chunks):
        snd[0, k] = jnp.dot(t_ref[k, other], d_ref[...], preferred_element_type=F32).astype(BF16)
        if k == 0:
            pl.semaphore_wait(barrier, H - 1 + N - 1)
        to_sib(0, k).start()

    def meet(g, k):
        to_sib(g, k).wait_recv()
        ybuf[g, k, y] = (own[k] + rcv[g, k].astype(F32)).astype(BF16)
        for j in range(1, Y):
            to_y(g, k, y, (y + j) % Y).start()

    for k in range(chunks):
        own[k] = jnp.dot(t_ref[k, core], d_ref[...], preferred_element_type=F32)
        meet(0, k)
    for k in range(chunks):
        for c in range(2):
            wide = t_ref[k, c].astype(F32)
            energy += jnp.sum(wide * wide)

    def joined(g, k):
        for j in range(1, Y):
            to_y(g, k, (y + j) % Y, (y + j) % Y).wait_recv()
        total = ybuf[g, k, 0].astype(F32)
        for yy in range(1, Y):
            total += ybuf[g, k, yy].astype(F32)
        buf = lat if g == 0 else dlat
        buf[k, core] = total.astype(BF16)
        back(g, k, core).start()

    def residual(k, c):
        r = t_ref[k, c].astype(F32) - jnp.dot(lat[k, c], u_ref[...], preferred_element_type=F32)
        res[k, c] = r.astype(BF16)
        return jnp.sum(r * r)

    misfit = jnp.zeros((), F32)
    for step in range(chunks + 2):
        k = step
        if k < chunks:
            joined(0, k)
        k = step - 1
        if 0 <= k < chunks:
            back(0, k, other).wait_recv()
            misfit += residual(k, other)
            snd[1, k] = nt(res[k, other], u_ref[...]).astype(BF16)
            to_sib(1, k).start()
            misfit += residual(k, core)
            own[k] = nt(res[k, core], u_ref[...])
        k = step - 2
        if 0 <= k < chunks:
            meet(1, k)

    tile = eh.shape[-2:]
    eh[h, 0] = jnp.full(tile, energy, F32)
    eh[h, 1] = jnp.full(tile, misfit, F32)

    def to_head(slot, hh):
        return remote(eh.at[slot], eh.at[slot], eh_send.at[hh], eh_recv.at[slot], (s, hh))

    def to_all(slot, ss):
        return remote(es.at[slot], es.at[slot], es_send.at[ss], es_recv.at[slot], (ss, h))

    for j in range(1, H):
        to_head(h, (h + j) % H).start()

    def scatter(g, grad):
        gsend[g] = grad.reshape(gsend.shape[1:]).astype(BF16)
        for j in range(1, N):
            ss = (s + j) % N
            to_seq(g, s, ss).start()

    scatter(0, tn(lat[...].reshape(-1, rank), res[...].reshape(-1, cols)))
    for j in range(1, H):
        hh = (h + j) % H
        to_head(hh, hh).wait_recv()
    total = eh[0]
    for hh in range(1, H):
        total += eh[hh]
    es[s] = total
    for j in range(1, N):
        to_all(s, (s + j) % N).start()

    for k in range(chunks + 1):
        if k < chunks:
            joined(1, k)
        if k == 0:
            continue
        back(1, k - 1, other).wait_recv()
        part = tn(dlat[k - 1].reshape(-1, rank), t_ref[k - 1].reshape(-1, cols))
        if k == 1:
            gacc[...] = part
        elif k < chunks:
            gacc[...] += part
        else:
            scatter(1, gacc[...] + part)

    for j in range(1, N):
        ss = (s + j) % N
        to_all(ss, ss).wait_recv()
    total = es[0]
    for ss in range(1, N):
        total += es[ss]
    whole_energy, whole_misfit = total[0], total[1]
    rel_ref[...] = whole_misfit / whole_energy
    factor = (-(entry_items / whole_energy) / math.sqrt(token_count))[0:1, 0:1]

    for g, out in ((0, gu_ref), (1, gd_ref)):
        total = gsend[g, s].astype(F32)
        for j in range(1, N):
            ss = (s + j) % N
            to_seq(g, ss, ss).wait_recv()
            total += grecv[g, ss].astype(F32)
        out[...] = factor * total

    for g in range(2):
        for k in range(chunks):
            to_sib(g, k).wait_send()
            back(g, k, core).wait_send()
            for j in range(1, Y):
                to_y(g, k, y, (y + j) % Y).wait_send()
        for j in range(1, N):
            to_seq(g, s, (s + j) % N).wait_send()
    for j in range(1, H):
        to_head(h, (h + j) % H).wait_send()
    for j in range(1, N):
        to_all(s, (s + j) % N).wait_send()


def tail(N, H, targets, down, up):
    rows, cols = targets.shape
    rank = down.shape[1]
    chunks = 4
    half = rows // chunks // 2
    block = rank // N
    Y = H // 2
    dma = pltpu.SemaphoreType.DMA
    vmem = pl.BlockSpec(memory_space=pltpu.VMEM)
    token_count = N * rows
    return pl.pallas_call(
        functools.partial(
            tail_kernel, N, H, token_count * 2 * KEY_VALUE_HEADS * HEAD_SIZE, token_count
        ),
        out_shape=(
            jax.ShapeDtypeStruct((block, cols), F32),
            jax.ShapeDtypeStruct((block, cols), F32),
            jax.ShapeDtypeStruct((8, 128), F32),
        ),
        in_specs=[vmem] * 3,
        out_specs=(vmem,) * 3,
        scratch_shapes=[
            pltpu.VMEM((2, chunks, half, rank), BF16),
            pltpu.VMEM((2, chunks, half, rank), BF16),
            pltpu.VMEM((chunks, half, rank), F32),
            pltpu.VMEM((rank, cols), F32),
            pltpu.VMEM((2, chunks, Y, half, rank), BF16),
            pltpu.VMEM((chunks, 2, half, rank), BF16),
            pltpu.VMEM((chunks, 2, half, rank), BF16),
            pltpu.VMEM((chunks, 2, half, cols), BF16),
            pltpu.VMEM((2, N, block, cols), BF16),
            pltpu.VMEM((2, N, block, cols), BF16),
            pltpu.VMEM((H, 2, 8, 128), F32),
            pltpu.VMEM((N, 2, 8, 128), F32),
            dma((2, 2, chunks)),
            dma((2, 2, chunks)),
            dma((2, chunks, Y)),
            dma((2, chunks, Y)),
            dma((2, N)),
            dma((2, N)),
            dma((H,)),
            dma((H,)),
            dma((N,)),
            dma((N,)),
        ],
        compiler_params=pltpu.CompilerParams(
            collective_id=1, has_side_effects=True, vmem_limit_bytes=48 * 2**20
        ),
    )(targets.reshape(chunks, 2, half, cols), down, up)


def solution(mesh):
    N, H = mesh.shape["seq"], mesh.shape["head"]

    def per_device(hidden, key_value_weight, down_projection, up_projection, positions):
        cosine, sine = rotation(positions)
        targets = gather_targets(N, hidden, key_value_weight, cosine, sine)
        grad_down, grad_up, rel = tail(N, H, targets, down_projection, up_projection)
        return grad_down, grad_up, rel[0, 0]

    return jax.shard_map(
        per_device,
        mesh=mesh,
        in_specs=(P("seq", None), P("seq", "head"), P("head", None), P(None, "head"), P("seq")),
        out_specs=(P("seq", "head"), P("seq", "head"), P()),
        check_vma=False,
    )
```

```python
import functools
import math

import jax
import jax.numpy as jnp
from jax import lax
from jax.experimental import pallas as pl
from jax.experimental.pallas import tpu as pltpu
from jax.sharding import PartitionSpec as P

KEY_VALUE_HEADS = 8
HEAD_SIZE = 128
THETA = 500000.0
MESH = pl.DeviceIdType.MESH
BF16 = jnp.bfloat16
F32 = jnp.float32


def rotation(positions):
    half_dim = HEAD_SIZE // 2
    freqs = jnp.power(
        jnp.float32(THETA), -(jnp.arange(half_dim, dtype=jnp.float32) * 2.0 / HEAD_SIZE)
    )
    angle = positions.astype(jnp.float32)[:, None] * freqs[None, :]
    cosine = jnp.cos(angle)
    sine = jnp.sin(angle)
    return (
        jnp.concatenate([cosine, cosine], axis=-1),
        jnp.concatenate([-sine, sine], axis=-1),
    )


def gather_kernel(
    A, B, chunks, groups, minor_first,
    hidden_ref, weight_ref, cos_ref, sin_ref, out_ref,
    hid, wbuf, acc, hid_sem, own_sem, send_sem, recv_sem,
):
    s, h = lax.axis_index("seq"), lax.axis_index("head")
    a, b = s // B, s % B
    depth = hid.shape[1] // (A * B)
    cols = weight_ref.shape[-1]
    load = pltpu.make_async_copy(hidden_ref, hid, hid_sem)
    load.start()
    own = pltpu.make_async_copy(weight_ref, wbuf.at[s], own_sem)
    own.start()

    barrier = pltpu.get_barrier_semaphore()
    ways = (
        (a + 1 < A, s + B),
        (a > 0, s - B),
        (b + 1 < B, s + 1),
        (b > 0, s - 1),
    )
    for there, peer in ways:
        @pl.when(there)
        def _():
            pl.semaphore_signal(barrier, inc=1, device_id=(peer, h), device_id_type=MESH)
    met = sum(there.astype(jnp.int32) for there, _ in ways)
    pl.semaphore_wait(barrier, met)

    def copy(way, peer, o, i):
        return pltpu.make_async_remote_copy(
            src_ref=wbuf.at[o, i],
            dst_ref=wbuf.at[o, i],
            send_sem=send_sem.at[way, o, i],
            recv_sem=recv_sem.at[o, i],
            device_id=(peer, h),
            device_id_type=MESH,
        )

    def forwards(da, db, o, i, act):
        first = i < minor_first
        conds = (
            (da >= 0) & (first | (db == 0)),
            (da <= 0) & (first | (db == 0)),
            (db >= 0) & (jnp.logical_not(first) | (da == 0)),
            (db <= 0) & (jnp.logical_not(first) | (da == 0)),
        )
        for way in range(4):
            @pl.when(ways[way][0] & conds[way])
            def _():
                act(copy(way, ways[way][1], o, i))

    piece = depth // groups
    span = chunks // groups

    def product(o, q):
        start = pl.multiple_of(o * depth + q * piece, piece)
        w = wbuf[o, pl.ds(q * span, span)].reshape(piece, cols)
        rows = 256
        def tile(m, c):
            r = pl.ds(pl.multiple_of(m * rows, rows), rows)
            acc[r, :] += jnp.dot(hid[r, pl.ds(start, piece)], w, preferred_element_type=F32)
            return c
        lax.fori_loop(0, hid.shape[0] // rows, tile, 0)

    own.wait()

    def issue(i, c):
        forwards(0, 0, s, i, lambda d: d.start())
        return c
    lax.fori_loop(0, chunks, issue, 0)
    acc[...] = jnp.zeros_like(acc)
    load.wait()

    def own_product(q, c):
        product(s, q)
        return c
    lax.fori_loop(0, groups, own_product, 0)

    def combos(u):
        for e in range(B):
            for eb in ((1, -1) if e else (1,)):
                for sa in (1, -1):
                    yield e * eb, u + 1 - e, sa

    def each(u, act):
        for off_b, d, sa in combos(u):
            a0, b0 = a + sa * d, b + off_b
            ok = (d >= 0) & (a0 >= 0) & (a0 < A) & (b0 >= 0) & (b0 < B)
            if sa < 0:
                ok = ok & (d > 0)

            @pl.when(ok)
            def _():
                act(a - a0, b - b0, a0 * B + b0)

    def stage(u, c):
        def group(q, c):
            def chunk(j, c):
                i = q * span + j

                def arrive(da, db, o):
                    copy(0, s, o, i).wait_recv()
                    forwards(da, db, o, i, lambda d: d.start())
                each(u, arrive)
                return c
            lax.fori_loop(0, span, chunk, 0)
            each(u, lambda da, db, o: product(o, q))
            return c
        return lax.fori_loop(0, groups, group, c)
    lax.fori_loop(0, A + B - 2, stage, 0)

    def finish(o, c):
        def chunk(i, c):
            forwards(a - o // B, b - o % B, o, i, lambda d: d.wait_send())
            return c
        return lax.fori_loop(0, chunks, chunk, c)
    lax.fori_loop(0, A * B, finish, 0)

    for head in range(cols // (2 * HEAD_SIZE)):
        k0 = head * 2 * HEAD_SIZE
        key = acc[:, k0 : k0 + HEAD_SIZE]
        turned = key * cos_ref[...] + pltpu.roll(key, HEAD_SIZE // 2, 1) * sin_ref[...]
        out_ref[:, k0 : k0 + HEAD_SIZE] = turned.astype(BF16)
        out_ref[:, k0 + HEAD_SIZE : k0 + 2 * HEAD_SIZE] = acc[
            :, k0 + HEAD_SIZE : k0 + 2 * HEAD_SIZE
        ].astype(BF16)


def gather_targets(N, hidden, weight, cosine, sine):
    B = 2 if N <= 8 else 8
    A = N // B
    rows, width = hidden.shape
    depth, cols = weight.shape
    chunks = 8 if N <= 8 else 2
    groups = max(1, depth // 256)
    minor_first = 1 if N <= 8 else 0
    shard = (chunks, depth // chunks, cols)
    return pl.pallas_call(
        functools.partial(gather_kernel, A, B, chunks, groups, minor_first),
        out_shape=jax.ShapeDtypeStruct((rows, cols), BF16),
        in_specs=[pl.BlockSpec(memory_space=pl.ANY)] * 2
        + [pl.BlockSpec(memory_space=pltpu.VMEM)] * 2,
        out_specs=pl.BlockSpec(memory_space=pltpu.VMEM),
        scratch_shapes=[
            pltpu.VMEM((rows, width), BF16),
            pltpu.VMEM((N,) + shard, BF16),
            pltpu.VMEM((rows, cols), F32),
            pltpu.SemaphoreType.DMA,
            pltpu.SemaphoreType.DMA,
            pltpu.SemaphoreType.DMA((4, N, chunks)),
            pltpu.SemaphoreType.DMA((N, chunks)),
        ],
        compiler_params=pltpu.CompilerParams(
            collective_id=0, has_side_effects=True, vmem_limit_bytes=50 * 2**20
        ),
    )(hidden, weight.reshape(shard), cosine, sine)


def tail_kernel(
    N, H, entry_items, token_count,
    t_ref, d_ref, u_ref, gd_ref, gu_ref, rel_ref,
    snd, rcv, own, gacc, ybuf, lat, dlat, res, gsend, grecv, eh, es,
    c_send, c_recv, y_send, y_recv, g_send, g_recv, eh_send, eh_recv, es_send, es_recv,
):
    s, h = lax.axis_index("seq"), lax.axis_index("head")
    Y = H // 2
    y, core = h // 2, h % 2
    other = 1 - core
    sib = y * 2 + other
    chunks, _, half, cols = t_ref.shape
    rank = d_ref.shape[1]

    barrier = pltpu.get_barrier_semaphore()
    for j in range(1, H):
        pl.semaphore_signal(barrier, inc=1, device_id=(s, (h + j) % H), device_id_type=MESH)
    for j in range(1, N):
        pl.semaphore_signal(barrier, inc=1, device_id=((s + j) % N, h), device_id_type=MESH)

    def remote(src, dst, ssem, rsem, peer):
        return pltpu.make_async_remote_copy(
            src_ref=src, dst_ref=dst, send_sem=ssem, recv_sem=rsem,
            device_id=peer, device_id_type=MESH,
        )

    def to_sib(g, k):
        return remote(snd.at[g, k], rcv.at[g, k], c_send.at[g, 0, k], c_recv.at[g, 0, k], (s, sib))

    def back(g, k, slot):
        buf = lat if g == 0 else dlat
        return remote(buf.at[k, slot], buf.at[k, slot], c_send.at[g, 1, k], c_recv.at[g, 1, k], (s, sib))

    def to_y(g, k, slot, yy):
        return remote(
            ybuf.at[g, k, slot], ybuf.at[g, k, slot], y_send.at[g, k, yy], y_recv.at[g, k, slot],
            (s, yy * 2 + core),
        )

    def to_seq(g, slot, ss):
        return remote(gsend.at[g, ss], grecv.at[g, slot], g_send.at[g, ss], g_recv.at[g, slot], (ss, h))

    def nt(x, w):
        return lax.dot_general(x, w, (((1,), (1,)), ((), ())), preferred_element_type=F32)

    def tn(x, w):
        return lax.dot_general(x, w, (((0,), (0,)), ((), ())), preferred_element_type=F32)

    energy = jnp.zeros((), F32)
    for k in range(chunks):
        snd[0, k] = jnp.dot(t_ref[k, other], d_ref[...], preferred_element_type=F32).astype(BF16)
        if k == 0:
            pl.semaphore_wait(barrier, H - 1 + N - 1)
        to_sib(0, k).start()

    def meet(g, k):
        to_sib(g, k).wait_recv()
        ybuf[g, k, y] = (own[k] + rcv[g, k].astype(F32)).astype(BF16)
        for j in range(1, Y):
            to_y(g, k, y, (y + j) % Y).start()

    for k in range(chunks):
        own[k] = jnp.dot(t_ref[k, core], d_ref[...], preferred_element_type=F32)
        meet(0, k)
    for k in range(chunks):
        for c in range(2):
            wide = t_ref[k, c].astype(F32)
            energy += jnp.sum(wide * wide)

    def joined(g, k):
        for j in range(1, Y):
            to_y(g, k, (y + j) % Y, (y + j) % Y).wait_recv()
        total = ybuf[g, k, 0].astype(F32)
        for yy in range(1, Y):
            total += ybuf[g, k, yy].astype(F32)
        buf = lat if g == 0 else dlat
        buf[k, core] = total.astype(BF16)
        back(g, k, core).start()

    def residual(k, c):
        r = t_ref[k, c].astype(F32) - jnp.dot(lat[k, c], u_ref[...], preferred_element_type=F32)
        res[k, c] = r.astype(BF16)
        return jnp.sum(r * r)

    misfit = jnp.zeros((), F32)
    for step in range(chunks + 2):
        k = step
        if k < chunks:
            joined(0, k)
        k = step - 1
        if 0 <= k < chunks:
            back(0, k, other).wait_recv()
            misfit += residual(k, other)
            snd[1, k] = nt(res[k, other], u_ref[...]).astype(BF16)
            to_sib(1, k).start()
            misfit += residual(k, core)
            own[k] = nt(res[k, core], u_ref[...])
        k = step - 2
        if 0 <= k < chunks:
            meet(1, k)

    tile = eh.shape[-2:]
    eh[h, 0] = jnp.full(tile, energy, F32)
    eh[h, 1] = jnp.full(tile, misfit, F32)

    def to_head(slot, hh):
        return remote(eh.at[slot], eh.at[slot], eh_send.at[hh], eh_recv.at[slot], (s, hh))

    def to_all(slot, ss):
        return remote(es.at[slot], es.at[slot], es_send.at[ss], es_recv.at[slot], (ss, h))

    for j in range(1, H):
        to_head(h, (h + j) % H).start()

    def scatter(g, grad):
        gsend[g] = grad.reshape(gsend.shape[1:]).astype(BF16)
        for j in range(1, N):
            ss = (s + j) % N
            to_seq(g, s, ss).start()

    scatter(0, tn(lat[...].reshape(-1, rank), res[...].reshape(-1, cols)))
    for j in range(1, H):
        hh = (h + j) % H
        to_head(hh, hh).wait_recv()
    total = eh[0]
    for hh in range(1, H):
        total += eh[hh]
    es[s] = total
    for j in range(1, N):
        to_all(s, (s + j) % N).start()

    for k in range(chunks + 1):
        if k < chunks:
            joined(1, k)
        if k == 0:
            continue
        back(1, k - 1, other).wait_recv()
        part = tn(dlat[k - 1].reshape(-1, rank), t_ref[k - 1].reshape(-1, cols))
        if k == 1:
            gacc[...] = part
        elif k < chunks:
            gacc[...] += part
        else:
            scatter(1, gacc[...] + part)

    for j in range(1, N):
        ss = (s + j) % N
        to_all(ss, ss).wait_recv()
    total = es[0]
    for ss in range(1, N):
        total += es[ss]
    whole_energy, whole_misfit = total[0], total[1]
    rel_ref[...] = whole_misfit / whole_energy
    factor = (-(entry_items / whole_energy) / math.sqrt(token_count))[0:1, 0:1]

    for g, out in ((0, gu_ref), (1, gd_ref)):
        total = gsend[g, s].astype(F32)
        for j in range(1, N):
            ss = (s + j) % N
            to_seq(g, ss, ss).wait_recv()
            total += grecv[g, ss].astype(F32)
        out[...] = factor * total

    for g in range(2):
        for k in range(chunks):
            to_sib(g, k).wait_send()
            back(g, k, core).wait_send()
            for j in range(1, Y):
                to_y(g, k, y, (y + j) % Y).wait_send()
        for j in range(1, N):
            to_seq(g, s, (s + j) % N).wait_send()
    for j in range(1, H):
        to_head(h, (h + j) % H).wait_send()
    for j in range(1, N):
        to_all(s, (s + j) % N).wait_send()


def tail(N, H, targets, down, up):
    rows, cols = targets.shape
    rank = down.shape[1]
    chunks = 4
    half = rows // chunks // 2
    block = rank // N
    Y = H // 2
    dma = pltpu.SemaphoreType.DMA
    vmem = pl.BlockSpec(memory_space=pltpu.VMEM)
    token_count = N * rows
    return pl.pallas_call(
        functools.partial(
            tail_kernel, N, H, token_count * 2 * KEY_VALUE_HEADS * HEAD_SIZE, token_count
        ),
        out_shape=(
            jax.ShapeDtypeStruct((block, cols), F32),
            jax.ShapeDtypeStruct((block, cols), F32),
            jax.ShapeDtypeStruct((8, 128), F32),
        ),
        in_specs=[vmem] * 3,
        out_specs=(vmem,) * 3,
        scratch_shapes=[
            pltpu.VMEM((2, chunks, half, rank), BF16),
            pltpu.VMEM((2, chunks, half, rank), BF16),
            pltpu.VMEM((chunks, half, rank), F32),
            pltpu.VMEM((rank, cols), F32),
            pltpu.VMEM((2, chunks, Y, half, rank), BF16),
            pltpu.VMEM((chunks, 2, half, rank), BF16),
            pltpu.VMEM((chunks, 2, half, rank), BF16),
            pltpu.VMEM((chunks, 2, half, cols), BF16),
            pltpu.VMEM((2, N, block, cols), BF16),
            pltpu.VMEM((2, N, block, cols), BF16),
            pltpu.VMEM((H, 2, 8, 128), F32),
            pltpu.VMEM((N, 2, 8, 128), F32),
            dma((2, 2, chunks)),
            dma((2, 2, chunks)),
            dma((2, chunks, Y)),
            dma((2, chunks, Y)),
            dma((2, N)),
            dma((2, N)),
            dma((H,)),
            dma((H,)),
            dma((N,)),
            dma((N,)),
        ],
        compiler_params=pltpu.CompilerParams(
            collective_id=1, has_side_effects=True, vmem_limit_bytes=48 * 2**20
        ),
    )(targets.reshape(chunks, 2, half, cols), down, up)


def solution(mesh):
    N, H = mesh.shape["seq"], mesh.shape["head"]

    def per_device(hidden, key_value_weight, down_projection, up_projection, positions):
        cosine, sine = rotation(positions)
        targets = gather_targets(N, hidden, key_value_weight, cosine, sine)
        grad_down, grad_up, rel = tail(N, H, targets, down_projection, up_projection)
        return grad_down, grad_up, rel[0, 0]

    return jax.shard_map(
        per_device,
        mesh=mesh,
        in_specs=(P("seq", None), P("seq", "head"), P("head", None), P(None, "head"), P("seq")),
        out_specs=(P("seq", "head"), P("seq", "head"), P()),
        check_vma=False,
    )
```

```python
import functools
import math

import jax
import jax.numpy as jnp
from jax import lax
from jax.experimental import pallas as pl
from jax.experimental.pallas import tpu as pltpu
from jax.sharding import PartitionSpec as P

KEY_VALUE_HEADS = 8
HEAD_SIZE = 128
THETA = 500000.0
MESH = pl.DeviceIdType.MESH
BF16 = jnp.bfloat16
F32 = jnp.float32


def rotation(positions):
    half_dim = HEAD_SIZE // 2
    freqs = jnp.power(
        jnp.float32(THETA), -(jnp.arange(half_dim, dtype=jnp.float32) * 2.0 / HEAD_SIZE)
    )
    angle = positions.astype(jnp.float32)[:, None] * freqs[None, :]
    cosine = jnp.cos(angle)
    sine = jnp.sin(angle)
    return (
        jnp.concatenate([cosine, cosine], axis=-1),
        jnp.concatenate([-sine, sine], axis=-1),
    )


def gather_kernel(
    A, B, chunks, groups, minor_first,
    hidden_ref, weight_ref, cos_ref, sin_ref, out_ref,
    hid, wbuf, acc, hid_sem, own_sem, send_sem, recv_sem,
):
    s, h = lax.axis_index("seq"), lax.axis_index("head")
    a, b = s // B, s % B
    depth = hid.shape[1] // (A * B)
    cols = weight_ref.shape[-1]
    load = pltpu.make_async_copy(hidden_ref, hid, hid_sem)
    load.start()
    own = pltpu.make_async_copy(weight_ref, wbuf.at[s], own_sem)
    own.start()

    barrier = pltpu.get_barrier_semaphore()
    ways = (
        (a + 1 < A, s + B),
        (a > 0, s - B),
        (b + 1 < B, s + 1),
        (b > 0, s - 1),
    )
    for there, peer in ways:
        @pl.when(there)
        def _():
            pl.semaphore_signal(barrier, inc=1, device_id=(peer, h), device_id_type=MESH)
    met = sum(there.astype(jnp.int32) for there, _ in ways)
    pl.semaphore_wait(barrier, met)

    def copy(way, peer, o, i):
        return pltpu.make_async_remote_copy(
            src_ref=wbuf.at[o, i],
            dst_ref=wbuf.at[o, i],
            send_sem=send_sem.at[way, o, i],
            recv_sem=recv_sem.at[o, i],
            device_id=(peer, h),
            device_id_type=MESH,
        )

    def forwards(da, db, o, i, act):
        first = i < minor_first
        conds = (
            (da >= 0) & (first | (db == 0)),
            (da <= 0) & (first | (db == 0)),
            (db >= 0) & (jnp.logical_not(first) | (da == 0)),
            (db <= 0) & (jnp.logical_not(first) | (da == 0)),
        )
        for way in range(4):
            @pl.when(ways[way][0] & conds[way])
            def _():
                act(copy(way, ways[way][1], o, i))

    piece = depth // groups
    span = chunks // groups

    def product(o, q):
        start = pl.multiple_of(o * depth + q * piece, piece)
        w = wbuf[o, pl.ds(q * span, span)].reshape(piece, cols)
        rows = 256
        def tile(m, c):
            r = pl.ds(pl.multiple_of(m * rows, rows), rows)
            acc[r, :] += jnp.dot(hid[r, pl.ds(start, piece)], w, preferred_element_type=F32)
            return c
        lax.fori_loop(0, hid.shape[0] // rows, tile, 0)

    own.wait()

    def issue(i, c):
        forwards(0, 0, s, i, lambda d: d.start())
        return c
    lax.fori_loop(0, chunks, issue, 0)
    acc[...] = jnp.zeros_like(acc)
    load.wait()

    def own_product(q, c):
        product(s, q)
        return c
    lax.fori_loop(0, groups, own_product, 0)

    def combos(u):
        for e in range(B):
            for eb in ((1, -1) if e else (1,)):
                for sa in (1, -1):
                    yield e * eb, u + 1 - e, sa

    def each(u, act):
        for off_b, d, sa in combos(u):
            a0, b0 = a + sa * d, b + off_b
            ok = (d >= 0) & (a0 >= 0) & (a0 < A) & (b0 >= 0) & (b0 < B)
            if sa < 0:
                ok = ok & (d > 0)

            @pl.when(ok)
            def _():
                act(a - a0, b - b0, a0 * B + b0)

    def stage(u, c):
        def group(q, c):
            def chunk(j, c):
                i = q * span + j

                def arrive(da, db, o):
                    copy(0, s, o, i).wait_recv()
                    forwards(da, db, o, i, lambda d: d.start())
                each(u, arrive)
                return c
            lax.fori_loop(0, span, chunk, 0)
            each(u, lambda da, db, o: product(o, q))
            return c
        lax.fori_loop(0, groups, group, 0)

        def sent(da, db, o):
            def chunk(i, c):
                forwards(da, db, o, i, lambda d: d.wait_send())
                return c
            lax.fori_loop(0, chunks, chunk, 0)
        each(u - 1, sent)
        return c
    lax.fori_loop(0, A + B - 2, stage, 0)

    for head in range(cols // (2 * HEAD_SIZE)):
        k0 = head * 2 * HEAD_SIZE
        key = acc[:, k0 : k0 + HEAD_SIZE]
        turned = key * cos_ref[...] + pltpu.roll(key, HEAD_SIZE // 2, 1) * sin_ref[...]
        out_ref[:, k0 : k0 + HEAD_SIZE] = turned.astype(BF16)
        out_ref[:, k0 + HEAD_SIZE : k0 + 2 * HEAD_SIZE] = acc[
            :, k0 + HEAD_SIZE : k0 + 2 * HEAD_SIZE
        ].astype(BF16)


def gather_targets(N, hidden, weight, cosine, sine):
    B = 2 if N <= 8 else 8
    A = N // B
    rows, width = hidden.shape
    depth, cols = weight.shape
    chunks = 8 if N <= 8 else 2
    groups = max(1, depth // 256)
    minor_first = 1 if N <= 8 else 0
    shard = (chunks, depth // chunks, cols)
    return pl.pallas_call(
        functools.partial(gather_kernel, A, B, chunks, groups, minor_first),
        out_shape=jax.ShapeDtypeStruct((rows, cols), BF16),
        in_specs=[pl.BlockSpec(memory_space=pl.ANY)] * 2
        + [pl.BlockSpec(memory_space=pltpu.VMEM)] * 2,
        out_specs=pl.BlockSpec(memory_space=pltpu.VMEM),
        scratch_shapes=[
            pltpu.VMEM((rows, width), BF16),
            pltpu.VMEM((N,) + shard, BF16),
            pltpu.VMEM((rows, cols), F32),
            pltpu.SemaphoreType.DMA,
            pltpu.SemaphoreType.DMA,
            pltpu.SemaphoreType.DMA((4, N, chunks)),
            pltpu.SemaphoreType.DMA((N, chunks)),
        ],
        compiler_params=pltpu.CompilerParams(
            collective_id=0, has_side_effects=True, vmem_limit_bytes=50 * 2**20
        ),
    )(hidden, weight.reshape(shard), cosine, sine)


def tail_kernel(
    N, H, entry_items, token_count,
    t_ref, d_ref, u_ref, gd_ref, gu_ref, rel_ref,
    snd, rcv, own, gacc, ybuf, lat, dlat, res, gsend, grecv, eh, es,
    c_send, c_recv, y_send, y_recv, g_send, g_recv, eh_send, eh_recv, es_send, es_recv,
):
    s, h = lax.axis_index("seq"), lax.axis_index("head")
    Y = H // 2
    y, core = h // 2, h % 2
    other = 1 - core
    sib = y * 2 + other
    chunks, _, half, cols = t_ref.shape
    rank = d_ref.shape[1]

    barrier = pltpu.get_barrier_semaphore()
    for j in range(1, H):
        pl.semaphore_signal(barrier, inc=1, device_id=(s, (h + j) % H), device_id_type=MESH)
    for j in range(1, N):
        pl.semaphore_signal(barrier, inc=1, device_id=((s + j) % N, h), device_id_type=MESH)

    def remote(src, dst, ssem, rsem, peer):
        return pltpu.make_async_remote_copy(
            src_ref=src, dst_ref=dst, send_sem=ssem, recv_sem=rsem,
            device_id=peer, device_id_type=MESH,
        )

    def to_sib(g, k):
        return remote(snd.at[g, k], rcv.at[g, k], c_send.at[g, 0, k], c_recv.at[g, 0, k], (s, sib))

    def back(g, k, slot):
        buf = lat if g == 0 else dlat
        return remote(buf.at[k, slot], buf.at[k, slot], c_send.at[g, 1, k], c_recv.at[g, 1, k], (s, sib))

    def to_y(g, k, slot, yy):
        return remote(
            ybuf.at[g, k, slot], ybuf.at[g, k, slot], y_send.at[g, k, yy], y_recv.at[g, k, slot],
            (s, yy * 2 + core),
        )

    def to_seq(g, slot, ss):
        return remote(gsend.at[g, ss], grecv.at[g, slot], g_send.at[g, ss], g_recv.at[g, slot], (ss, h))

    def nt(x, w):
        return lax.dot_general(x, w, (((1,), (1,)), ((), ())), preferred_element_type=F32)

    def tn(x, w):
        return lax.dot_general(x, w, (((0,), (0,)), ((), ())), preferred_element_type=F32)

    energy = jnp.zeros((), F32)
    for k in range(chunks):
        snd[0, k] = jnp.dot(t_ref[k, other], d_ref[...], preferred_element_type=F32).astype(BF16)
        if k == 0:
            pl.semaphore_wait(barrier, H - 1 + N - 1)
        to_sib(0, k).start()

    def meet(g, k):
        to_sib(g, k).wait_recv()
        ybuf[g, k, y] = (own[k] + rcv[g, k].astype(F32)).astype(BF16)
        for j in range(1, Y):
            to_y(g, k, y, (y + j) % Y).start()

    for k in range(chunks):
        own[k] = jnp.dot(t_ref[k, core], d_ref[...], preferred_element_type=F32)
        meet(0, k)
    for k in range(chunks):
        for c in range(2):
            wide = t_ref[k, c].astype(F32)
            energy += jnp.sum(wide * wide)

    def joined(g, k):
        for j in range(1, Y):
            to_y(g, k, (y + j) % Y, (y + j) % Y).wait_recv()
        total = ybuf[g, k, 0].astype(F32)
        for yy in range(1, Y):
            total += ybuf[g, k, yy].astype(F32)
        buf = lat if g == 0 else dlat
        buf[k, core] = total.astype(BF16)
        back(g, k, core).start()

    def residual(k, c):
        r = t_ref[k, c].astype(F32) - jnp.dot(lat[k, c], u_ref[...], preferred_element_type=F32)
        res[k, c] = r.astype(BF16)
        return jnp.sum(r * r)

    misfit = jnp.zeros((), F32)
    for step in range(chunks + 2):
        k = step
        if k < chunks:
            joined(0, k)
        k = step - 1
        if 0 <= k < chunks:
            back(0, k, other).wait_recv()
            misfit += residual(k, other)
            snd[1, k] = nt(res[k, other], u_ref[...]).astype(BF16)
            to_sib(1, k).start()
            misfit += residual(k, core)
            own[k] = nt(res[k, core], u_ref[...])
        k = step - 2
        if 0 <= k < chunks:
            meet(1, k)

    tile = eh.shape[-2:]
    eh[h, 0] = jnp.full(tile, energy, F32)
    eh[h, 1] = jnp.full(tile, misfit, F32)

    def to_head(slot, hh):
        return remote(eh.at[slot], eh.at[slot], eh_send.at[hh], eh_recv.at[slot], (s, hh))

    def to_all(slot, ss):
        return remote(es.at[slot], es.at[slot], es_send.at[ss], es_recv.at[slot], (ss, h))

    for j in range(1, H):
        to_head(h, (h + j) % H).start()

    def scatter(g, grad):
        gsend[g] = grad.reshape(gsend.shape[1:]).astype(BF16)
        for j in range(1, N):
            ss = (s + j) % N
            to_seq(g, s, ss).start()

    scatter(0, tn(lat[...].reshape(-1, rank), res[...].reshape(-1, cols)))
    for j in range(1, H):
        hh = (h + j) % H
        to_head(hh, hh).wait_recv()
    total = eh[0]
    for hh in range(1, H):
        total += eh[hh]
    es[s] = total
    for j in range(1, N):
        to_all(s, (s + j) % N).start()

    for k in range(chunks + 1):
        if k < chunks:
            joined(1, k)
        if k == 0:
            continue
        back(1, k - 1, other).wait_recv()
        part = tn(dlat[k - 1].reshape(-1, rank), t_ref[k - 1].reshape(-1, cols))
        if k == 1:
            gacc[...] = part
        elif k < chunks:
            gacc[...] += part
        else:
            scatter(1, gacc[...] + part)

    for j in range(1, N):
        ss = (s + j) % N
        to_all(ss, ss).wait_recv()
    total = es[0]
    for ss in range(1, N):
        total += es[ss]
    whole_energy, whole_misfit = total[0], total[1]
    rel_ref[...] = whole_misfit / whole_energy
    factor = (-(entry_items / whole_energy) / math.sqrt(token_count))[0:1, 0:1]

    for g, out in ((0, gu_ref), (1, gd_ref)):
        total = gsend[g, s].astype(F32)
        for j in range(1, N):
            ss = (s + j) % N
            to_seq(g, ss, ss).wait_recv()
            total += grecv[g, ss].astype(F32)
        out[...] = factor * total

    for g in range(2):
        for k in range(chunks):
            to_sib(g, k).wait_send()
            back(g, k, core).wait_send()
            for j in range(1, Y):
                to_y(g, k, y, (y + j) % Y).wait_send()
        for j in range(1, N):
            to_seq(g, s, (s + j) % N).wait_send()
    for j in range(1, H):
        to_head(h, (h + j) % H).wait_send()
    for j in range(1, N):
        to_all(s, (s + j) % N).wait_send()


def tail(N, H, targets, down, up):
    rows, cols = targets.shape
    rank = down.shape[1]
    chunks = 4
    half = rows // chunks // 2
    block = rank // N
    Y = H // 2
    dma = pltpu.SemaphoreType.DMA
    vmem = pl.BlockSpec(memory_space=pltpu.VMEM)
    token_count = N * rows
    return pl.pallas_call(
        functools.partial(
            tail_kernel, N, H, token_count * 2 * KEY_VALUE_HEADS * HEAD_SIZE, token_count
        ),
        out_shape=(
            jax.ShapeDtypeStruct((block, cols), F32),
            jax.ShapeDtypeStruct((block, cols), F32),
            jax.ShapeDtypeStruct((8, 128), F32),
        ),
        in_specs=[vmem] * 3,
        out_specs=(vmem,) * 3,
        scratch_shapes=[
            pltpu.VMEM((2, chunks, half, rank), BF16),
            pltpu.VMEM((2, chunks, half, rank), BF16),
            pltpu.VMEM((chunks, half, rank), F32),
            pltpu.VMEM((rank, cols), F32),
            pltpu.VMEM((2, chunks, Y, half, rank), BF16),
            pltpu.VMEM((chunks, 2, half, rank), BF16),
            pltpu.VMEM((chunks, 2, half, rank), BF16),
            pltpu.VMEM((chunks, 2, half, cols), BF16),
            pltpu.VMEM((2, N, block, cols), BF16),
            pltpu.VMEM((2, N, block, cols), BF16),
            pltpu.VMEM((H, 2, 8, 128), F32),
            pltpu.VMEM((N, 2, 8, 128), F32),
            dma((2, 2, chunks)),
            dma((2, 2, chunks)),
            dma((2, chunks, Y)),
            dma((2, chunks, Y)),
            dma((2, N)),
            dma((2, N)),
            dma((H,)),
            dma((H,)),
            dma((N,)),
            dma((N,)),
        ],
        compiler_params=pltpu.CompilerParams(
            collective_id=1, has_side_effects=True, vmem_limit_bytes=48 * 2**20
        ),
    )(targets.reshape(chunks, 2, half, cols), down, up)


def solution(mesh):
    N, H = mesh.shape["seq"], mesh.shape["head"]

    def per_device(hidden, key_value_weight, down_projection, up_projection, positions):
        cosine, sine = rotation(positions)
        targets = gather_targets(N, hidden, key_value_weight, cosine, sine)
        grad_down, grad_up, rel = tail(N, H, targets, down_projection, up_projection)
        return grad_down, grad_up, rel[0, 0]

    return jax.shard_map(
        per_device,
        mesh=mesh,
        in_specs=(P("seq", None), P("seq", "head"), P("head", None), P(None, "head"), P("seq")),
        out_specs=(P("seq", "head"), P("seq", "head"), P()),
        check_vma=False,
    )
```
